512 devices in a mesh: dp: 32 (over y_lo, x, core), shard: 16 (over y_hi, z).
Axes of the slice: x: 4, y: 8 (y_hi: 2, y_lo: 4; y = y_hi * 4 + y_lo), z: 8, core: 2. Of those that a mesh axis runs over, the one named last changes fastest.
Arguments:
- tokens: bfloat16 [32768, 8192], P('dp', 'shard'), may hold values from -6 to 6
- weight_t: bfloat16 [1024, 8192], P('dp', 'shard'), may hold values from -0.0625 to 0.0625
- cotangent: bfloat16 [32768, 1024], P('dp'), may hold values from -6 to 6
- hard_ids: int32 [32, 8], P('dp'), may hold values from 0 to 7, each once within a row
- hard_count: int32 [32], replicated, may hold values from 0 to 8, as said below
Outputs:
- kv_rows: bfloat16 [32768, 1024], P(('dp', 'shard'))
- token_grad: bfloat16 [32768, 8192], P('dp', 'shard')
- weight_grad: float32 [1024, 8192], P('dp', 'shard')
The draws below stay inside these ranges and needn't reach their ends.
Inputs may be any that keep to these rules, and one draw needn't show every extreme that they name: `hard_count`: the counts sum to 128; in every draw one group has 8 hard sequences and another none.
All inputs are finite; a program needn't handle non-finite values.
Results may differ from the reference program's by a relative error of at most 0.022.
Values may be sent and summed in bfloat16 or wider, within the bound.
A program may use at most 64 MiB of HBM per device.

```python
import math
import jax
import jax.numpy as jnp
from jax import lax

D = 8192
C = 1024
SEQS = 8
L = 128
GROUPS = 32
HARD_DEV = 4
TOKENS = 32768
N_SHARD = 16


def draw_hard_count(key, part):
    half = SEQS // 2
    order = jax.random.permutation(jax.random.fold_in(key, 11), GROUPS)
    offsets = jax.random.randint(jax.random.fold_in(key, 12), (GROUPS // 2,), 0, half + 1)
    offsets = offsets.at[0].set(half)
    counts = jnp.zeros((GROUPS,), jnp.int32)
    counts = counts.at[order[0::2]].set(half + offsets)
    counts = counts.at[order[1::2]].set(half - offsets)
    return counts.astype(jnp.int32)


def with_spikes(drawn, key, source, target, blocks, factor):
    owner, partner = [(jnp.arange(drawn.shape[position]) // (drawn.shape[position] // blocks)).reshape([-1 if axis == position else 1 for axis in range(drawn.ndim)]) for position in (source, target)]
    chosen = jax.random.permutation(key, blocks)[partner]
    strong = (owner == chosen) | (owner == (partner + blocks // 2) % blocks)
    return jnp.where(strong, factor * drawn, drawn)


def block_scale(key, extent, pieces, smallest, largest):
    loudness = 1.0
    for position, blocks in pieces:
        steps = jax.random.uniform(jax.random.fold_in(jax.random.fold_in(key, 6), position), (blocks,), jnp.float32, smallest / len(pieces), largest / len(pieces))
        loudness = loudness * jnp.repeat(jnp.exp(steps), extent[position] // blocks).reshape((-1,) + (1,) * (len(extent) - 1 - position))
    return loudness


def centred(key, dims, scale, reach, pieces=(), kind=jnp.bfloat16):
    loudness = block_scale(key, dims, pieces, -0.22, 0.18) if pieces else 1.0
    entries = jax.random.normal(key, dims, jnp.float32) * scale * loudness
    return jnp.minimum(jnp.maximum(entries, -reach), reach).astype(kind)


def noise_with(own_key, extent, scale, bound, split, heavy, held_as=jnp.bfloat16):
    drawn = scale * jax.random.normal(own_key, extent, jnp.float32)
    if split:
        drawn = drawn * block_scale(own_key, extent, split, -0.22, 0.18)
    return jnp.clip(with_spikes(drawn, jax.random.fold_in(own_key, 3), *heavy), -bound, bound).astype(held_as)


def setup_inputs(seed: int = 0) -> dict:
    key_list = jax.random.split(jax.random.key(seed), 6)
    return {
        "tokens": centred(key_list[0], (TOKENS, D), 1.0, 6.0, ((0, 32), (1, 16))),
        "weight_t": centred(key_list[1], (C, D), D ** -0.5, 0.0625, ((0, 32), (1, 16))),
        "cotangent": noise_with(key_list[2], (TOKENS, C), 1.0, 6.0, ((0, 32),), (0, 1, 32, 2.75)),
        "hard_ids": jax.vmap(lambda own: jax.random.permutation(own, SEQS))(jax.random.split(key_list[3], GROUPS)).reshape((GROUPS, SEQS)).astype(jnp.int32),
        "hard_count": draw_hard_count(jax.random.fold_in(key_list[5], 71), 0),
    }


def reference(tokens, weight_t, cotangent, hard_ids, hard_count):
    width = tokens.shape[1]
    chans = weight_t.shape[0]
    block = width // N_SHARD
    token_blocks = tokens.reshape(tokens.shape[0], N_SHARD, block).transpose(1, 0, 2)
    weight_blocks = weight_t.reshape(chans, N_SHARD, block).transpose(1, 0, 2)

    def add_block(total, pair):
        part_rows, part_weight = pair
        partial_value = jnp.dot(part_rows, part_weight.T, preferred_element_type=jnp.float32).astype(jnp.bfloat16)
        partial_value = lax.optimization_barrier(partial_value)
        return (total + partial_value.astype(jnp.float32), None)
    start_total = jnp.zeros((tokens.shape[0], chans), jnp.float32)
    kv_total, _ = lax.scan(add_block, start_total, (token_blocks, weight_blocks))
    kv_rows = kv_total.astype(jnp.bfloat16)
    grouped = tokens.reshape(GROUPS, SEQS, L, width)
    picked = jax.vmap(lambda rows_in, order: jnp.take(rows_in, order, axis=0))(grouped, hard_ids)
    live = jnp.arange(SEQS, dtype=jnp.int32)[None, :] < hard_count[:, None]
    picked = jnp.where(live[:, :, None, None], picked, jnp.zeros_like(picked)).reshape(-1, width)
    grads = cotangent.reshape(GROUPS, SEQS, L, chans)
    grads = jnp.where(live[:, :, None, None], grads, jnp.zeros_like(grads)).reshape(-1, chans)
    token_grad = jnp.dot(grads, weight_t, preferred_element_type=jnp.float32).astype(jnp.bfloat16)
    factor = 1.0 / math.sqrt(GROUPS * HARD_DEV * L)
    weight_grad = lax.dot_general(grads, picked, (((0,), (0,)), ((), ())), preferred_element_type=jnp.float32) * factor
    return (kv_rows, token_grad, weight_grad)
```

```python
import math

import jax
import jax.numpy as jnp
from jax import lax
from jax.experimental import pallas as pl
from jax.experimental.pallas import tpu as pltpu
from jax.sharding import PartitionSpec as P

SEQS = 8
L = 128
HARD_DEV = 4
CHUNKS = 4
NT = (((1,), (1,)), ((), ()))
TN = (((0,), (0,)), ((), ()))
F32 = jnp.float32
BF16 = jnp.bfloat16


def send(src, dst, send_sem, recv_sem, device):
    copy = pltpu.make_async_remote_copy(
        src_ref=src,
        dst_ref=dst,
        send_sem=send_sem,
        recv_sem=recv_sem,
        device_id=device,
        device_id_type=pl.DeviceIdType.MESH,
    )
    copy.start()
    return copy


def kernel(
    factor,
    ids,
    count,
    tok_hbm,
    w_hbm,
    cot_hbm,
    kv_out,
    tg_hbm,
    wg_out,
    tok,
    cot,
    w,
    pick,
    part,
    from_left,
    from_right,
    both,
    kept,
    from_half,
    grad,
    from_core,
    x1,
    x2r,
    x2l,
    ysum,
    from_y,
    tg,
    load_sem,
    tg_sem,
    w_send,
    w_recv,
    z_send,
    z_recv,
    h_send,
    h_recv,
    c_send,
    c_recv,
    x1_send,
    x1_recv,
    x2_send,
    x2_recv,
    y_send,
    y_recv,
):
    d = lax.axis_index("dp")
    s = lax.axis_index("shard")
    c = d % 2
    x = (d // 2) % 4
    y = d // 8
    z = s % 8
    half = s // 8
    xr, xl, xo = (x + 1) % 4, (x + 3) % 4, (x + 2) % 4
    right = (d, half * 8 + (z + 1) % 8)
    left = (d, half * 8 + (z + 7) % 8)
    other_half = (d, (1 - half) * 8 + z)

    def at(yy, xx, cc):
        return (yy * 4 + xx) * 2 + cc

    core = (at(y, x, 1 - c), s)
    x_right = (at(y, xr, c), s)
    x_left = (at(y, xl, c), s)
    ys = [(y + k) % 4 for k in range(4)]
    y_peers = [(at(ys[k], x, c), s) for k in range(1, 4)]

    barrier = pltpu.get_barrier_semaphore()
    peers = [*y_peers, x_right, x_left, core, right, left, other_half]
    for peer in peers:
        pl.semaphore_signal(barrier, inc=1, device_id=peer, device_id_type=pl.DeviceIdType.MESH)

    def block(index):
        return w.at[pl.ds(pl.multiple_of(index * 32, 32), 32), :]

    loads = [
        pltpu.make_async_copy(w_hbm, block(d), load_sem.at[0]),
        pltpu.make_async_copy(tok_hbm, tok, load_sem.at[1]),
        pltpu.make_async_copy(cot_hbm, cot, load_sem.at[2]),
    ]
    for load in loads:
        load.start()
    loads[0].wait()
    pl.semaphore_wait(barrier, len(peers))

    sent = []

    def w_to(index, device):
        sent.append(send(block(index), block(index), w_send.at[len(sent)], w_recv.at[index], device))

    def w_wait(index):
        pltpu.make_async_remote_copy(
            src_ref=block(index),
            dst_ref=block(index),
            send_sem=w_send.at[0],
            recv_sem=w_recv.at[index],
            device_id=core,
            device_id_type=pl.DeviceIdType.MESH,
        ).wait_recv()

    for peer in reversed(y_peers):
        w_to(d, peer)
    for peer in (x_right, x_left, core):
        w_to(d, peer)

    own_count = count[d]

    def live(k):
        return jnp.clip(own_count - k, 0, 1).astype(F32)

    loads[1].wait()
    for k in range(SEQS):
        rows = tok[ids[0, k]].astype(F32) * live(k)
        pick[k * L : (k + 1) * L, :] = rows.astype(BF16)
    loads[2].wait()

    c_copies = []

    def grad_piece(j):
        product = lax.dot_general(
            cot[:, j * 256 : (j + 1) * 256], pick[...], TN, preferred_element_type=F32
        )
        product = (product * factor).astype(BF16).reshape(4, 2, 32, 512)
        for cc in range(2):
            grad[cc, j] = product[:, cc]
        c_copies.append(
            send(grad.at[1 - c, j], from_core.at[j], c_send.at[j], c_recv.at[j], core)
        )

    grad_piece(0)
    for k in range(1, 4):
        w_wait(at(ys[k], x, c))
        for peer in (x_right, x_left, core):
            w_to(at(ys[k], x, c), peer)
    grad_piece(1)
    for k in range(4):
        from_l, from_r = at(ys[k], xl, c), at(ys[k], xr, c)
        w_wait(from_l)
        if k < 2:
            w_to(from_l, x_right)
        w_to(from_l, core)
        w_wait(from_r)
        if k >= 2:
            w_to(from_r, x_left)
        w_to(from_r, core)
    for k in range(4):
        w_wait(at(ys[k], xo, c))
        w_to(at(ys[k], xo, c), core)
    for yy in range(4):
        for xx in range(4):
            w_wait(at(yy, xx, 1 - c))

    width = 1024 // CHUNKS
    z_copies = {}
    h_copies = []

    def z_right(j, r, src, dst):
        z_copies[0, j, r] = send(src, dst, z_send.at[0, j, r], z_recv.at[0, j, r], right)

    def z_left(j, r, src, dst):
        z_copies[1, j, r] = send(src, dst, z_send.at[1, j, r], z_recv.at[1, j, r], left)

    def start_chunk(j):
        for h in range(2):
            product = lax.dot_general(
                tok[h * 4 : (h + 1) * 4].reshape(512, 512),
                w[j * width : (j + 1) * width, :],
                NT,
                preferred_element_type=F32,
            )
            part[j, :, h] = product.astype(BF16).reshape(8, 64, width)
        far = (z + 4) % 8
        z_right(j, 0, part.at[j, far, 0], from_left.at[j, 0, 0])
        z_left(j, 0, part.at[j, far, 1], from_right.at[j, 0, 1])

    def add_into(ref, index, other):
        ref[index] = (ref[index].astype(F32) + other.astype(F32)).astype(BF16)

    def z_round(j, r):
        to_right, to_left = (z + 4 - r) % 8, (z + 4 + r) % 8
        z_copies[0, j, r - 1].wait_recv()
        if r == 1:
            add_into(part, (j, to_right, 0), from_left[j, 0, 0])
        else:
            add_into(part, (j, to_right), from_left[j, r - 1])
        z_right(j, r, part.at[j, to_right], from_left.at[j, r])
        z_copies[1, j, r - 1].wait_recv()
        if r == 1:
            add_into(part, (j, to_left, 1), from_right[j, 0, 1])
        else:
            add_into(part, (j, to_left), from_right[j, r - 1])
        z_left(j, r, part.at[j, to_left], from_right.at[j, r])

    def z_finish(j):
        z_copies[0, j, 3].wait_recv()
        z_copies[1, j, 3].wait_recv()
        total = part[j, z].astype(F32) + from_left[j, 3].astype(F32) + from_right[j, 3].astype(F32)
        kept[j] = total
        both[j] = total.astype(BF16)
        h_copies.append(
            send(both.at[j, 1 - half], from_half.at[j], h_send.at[j], h_recv.at[j], other_half)
        )

    def kv_finish(j):
        h_copies[j].wait_recv()
        total = kept[j, half] + from_half[j].astype(F32)
        kv_out[:, j * width : (j + 1) * width] = total.astype(BF16)

    x1_copies = {}
    x2_copies = {}
    y_copies = []

    def grad_core():
        for j in range(4):
            c_copies[j].wait_recv()
            add_into(grad, (c, j), from_core[j])
        for j in range(4):
            x1_copies[j] = send(
                grad.at[c, j, xo],
                x1.at[j],
                x1_send.at[j],
                x1_recv.at[j],
                x_right if j < 2 else x_left,
            )
        for j in (2, 3):
            x2_copies[0, j] = send(
                grad.at[c, j, xr], x2r.at[j], x2_send.at[0, j], x2_recv.at[0, j], x_right
            )
        for j in (0, 1):
            x2_copies[1, j] = send(
                grad.at[c, j, xl], x2l.at[j], x2_send.at[1, j], x2_recv.at[1, j], x_left
            )

    def grad_x():
        for j in range(2):
            x1_copies[j].wait_recv()
            add_into(grad, (c, j, xr), x1[j])
            x2_copies[0, j] = send(
                grad.at[c, j, xr], x2r.at[j], x2_send.at[0, j], x2_recv.at[0, j], x_right
            )
        for j in range(2, 4):
            x1_copies[j].wait_recv()
            add_into(grad, (c, j, xl), x1[j])
            x2_copies[1, j] = send(
                grad.at[c, j, xl], x2l.at[j], x2_send.at[1, j], x2_recv.at[1, j], x_left
            )

    def grad_y():
        for j in range(4):
            x2_copies[0, j].wait_recv()
            x2_copies[1, j].wait_recv()
        for j in range(4):
            total = grad[c, j, x].astype(F32) + x2r[j].astype(F32) + x2l[j].astype(F32)
            ysum[j] = total.astype(BF16)
        for k in range(1, 4):
            y_copies.append(
                send(
                    ysum.at[ys[k]],
                    from_y.at[k - 1],
                    y_send.at[k - 1],
                    y_recv.at[k - 1],
                    y_peers[k - 1],
                )
            )

    def grad_finish():
        total = ysum[y].astype(F32)
        for k in range(3):
            y_copies[k].wait_recv()
            total = total + from_y[k].astype(F32)
        wg_out[...] = total

    tg_copies = []

    def token_piece(p):
        rows = slice(p * 256, (p + 1) * 256)
        product = jnp.dot(cot[rows, :], w[...], preferred_element_type=F32)
        for i in range(2):
            own = product[i * L : (i + 1) * L] * live(2 * p + i)
            tg[p * 256 + i * L : p * 256 + (i + 1) * L, :] = own.astype(BF16)
        copy = pltpu.make_async_copy(tg.at[rows, :], tg_hbm.at[rows, :], tg_sem.at[p])
        copy.start()
        tg_copies.append(copy)

    beside = {
        0: [lambda: grad_piece(2)],
        1: [lambda: grad_piece(3), grad_core],
        2: [grad_x, lambda: token_piece(0)],
        3: [grad_y, lambda: token_piece(1)],
        4: [grad_finish, lambda: token_piece(2)],
        5: [lambda: token_piece(3)],
    }
    for t in range(CHUNKS + 6):
        if t < CHUNKS:
            start_chunk(t)
        for r in (4, 3, 2, 1):
            j = t - r
            if 0 <= j < CHUNKS:
                if r == 4:
                    z_finish(j)
                else:
                    z_round(j, r)
        for extra in beside.get(t, []):
            extra()
        if 0 <= t - 6 < CHUNKS:
            kv_finish(t - 6)

    everything = [*sent, *c_copies, *z_copies.values(), *h_copies]
    everything += [*x1_copies.values(), *x2_copies.values(), *y_copies]
    for copy in everything:
        copy.wait_send()
    for copy in tg_copies:
        copy.wait()


def per_device(tokens, weight_t, cotangent, hard_ids, hard_count):
    factor = 1.0 / math.sqrt(lax.axis_size("dp") * HARD_DEV * L)
    rows, width = tokens.shape
    chans = cotangent.shape[1]
    wide = chans // CHUNKS
    any_spec = pl.BlockSpec(memory_space=pl.ANY)
    smem = pl.BlockSpec(memory_space=pltpu.SMEM)
    vmem = pl.BlockSpec(memory_space=pltpu.VMEM)
    dma = pltpu.SemaphoreType.DMA

    def body(*refs):
        kernel(factor, *refs)

    return pl.pallas_call(
        body,
        out_shape=(
            jax.ShapeDtypeStruct((64, chans), BF16),
            jax.ShapeDtypeStruct((rows, width), BF16),
            jax.ShapeDtypeStruct((32, width), F32),
        ),
        in_specs=[smem, smem, any_spec, any_spec, any_spec],
        out_specs=(vmem, any_spec, vmem),
        scratch_shapes=[
            pltpu.VMEM((SEQS, L, width), BF16),
            pltpu.VMEM((rows, chans), BF16),
            pltpu.VMEM((chans, width), BF16),
            pltpu.VMEM((rows, width), BF16),
            pltpu.VMEM((CHUNKS, 8, 2, 64, wide), BF16),
            pltpu.VMEM((CHUNKS, 4, 2, 64, wide), BF16),
            pltpu.VMEM((CHUNKS, 4, 2, 64, wide), BF16),
            pltpu.VMEM((CHUNKS, 2, 64, wide), BF16),
            pltpu.VMEM((CHUNKS, 2, 64, wide), F32),
            pltpu.VMEM((CHUNKS, 64, wide), BF16),
            pltpu.VMEM((2, 4, 4, 32, width), BF16),
            pltpu.VMEM((4, 4, 32, width), BF16),
            pltpu.VMEM((4, 32, width), BF16),
            pltpu.VMEM((4, 32, width), BF16),
            pltpu.VMEM((4, 32, width), BF16),
            pltpu.VMEM((4, 32, width), BF16),
            pltpu.VMEM((3, 32, width), BF16),
            pltpu.VMEM((rows, width), BF16),
            dma((3,)),
            dma((4,)),
            dma((40,)),
            dma((32,)),
            dma((2, CHUNKS, 4)),
            dma((2, CHUNKS, 4)),
            dma((CHUNKS,)),
            dma((CHUNKS,)),
            dma((4,)),
            dma((4,)),
            dma((4,)),
            dma((4,)),
            dma((2, 4)),
            dma((2, 4)),
            dma((3,)),
            dma((3,)),
        ],
        compiler_params=pltpu.CompilerParams(collective_id=0, has_side_effects=True),
    )(hard_ids, hard_count, tokens.reshape(SEQS, L, width), weight_t, cotangent)


def solution(mesh):
    return jax.shard_map(
        per_device,
        mesh=mesh,
        in_specs=(P("dp", "shard"), P("dp", "shard"), P("dp", None), P("dp", None), P()),
        out_specs=(P(("dp", "shard"), None), P("dp", "shard"), P("dp", "shard")),
        check_vma=False,
    )
```

```python
import math

import jax
import jax.numpy as jnp
from jax import lax
from jax.experimental import pallas as pl
from jax.experimental.pallas import tpu as pltpu
from jax.sharding import PartitionSpec as P

SEQS = 8
L = 128
HARD_DEV = 4
CHUNKS = 4
NT = (((1,), (1,)), ((), ()))
TN = (((0,), (0,)), ((), ()))
F32 = jnp.float32
BF16 = jnp.bfloat16


def send(src, dst, send_sem, recv_sem, device):
    copy = pltpu.make_async_remote_copy(
        src_ref=src,
        dst_ref=dst,
        send_sem=send_sem,
        recv_sem=recv_sem,
        device_id=device,
        device_id_type=pl.DeviceIdType.MESH,
    )
    copy.start()
    return copy


def kernel(
    factor,
    ids,
    count,
    tok_hbm,
    w_hbm,
    cot_hbm,
    kv_out,
    tg_hbm,
    wg_out,
    tok,
    cot,
    w,
    pick,
    part,
    from_left,
    from_right,
    both,
    kept,
    from_half,
    grad,
    from_core,
    x1,
    x2r,
    x2l,
    ysum,
    from_y,
    tg,
    load_sem,
    tg_sem,
    w_send,
    f_send,
    w_recv,
    z_send,
    z_recv,
    h_send,
    h_recv,
    c_send,
    c_recv,
    x1_send,
    x1_recv,
    x2_send,
    x2_recv,
    y_send,
    y_recv,
):
    d = lax.axis_index("dp")
    s = lax.axis_index("shard")
    c = d % 2
    x = (d // 2) % 4
    y = d // 8
    z = s % 8
    half = s // 8
    xr, xl, xo = (x + 1) % 4, (x + 3) % 4, (x + 2) % 4
    right = (d, half * 8 + (z + 1) % 8)
    left = (d, half * 8 + (z + 7) % 8)
    other_half = (d, (1 - half) * 8 + z)

    def at(yy, xx, cc):
        return (yy * 4 + xx) * 2 + cc

    core = (at(y, x, 1 - c), s)
    x_right = (at(y, xr, c), s)
    x_left = (at(y, xl, c), s)
    ys = [(y + k) % 4 for k in range(4)]
    y_peers = [(at(ys[k], x, c), s) for k in range(1, 4)]

    barrier = pltpu.get_barrier_semaphore()
    peers = [*y_peers, x_right, x_left, core, right, left, other_half]
    for peer in peers:
        pl.semaphore_signal(barrier, inc=1, device_id=peer, device_id_type=pl.DeviceIdType.MESH)

    def block(index):
        return w.at[pl.ds(pl.multiple_of(index * 32, 32), 32), :]

    loads = [
        pltpu.make_async_copy(w_hbm, block(d), load_sem.at[0]),
        pltpu.make_async_copy(tok_hbm, tok, load_sem.at[1]),
        pltpu.make_async_copy(cot_hbm, cot, load_sem.at[2]),
    ]
    for load in loads:
        load.start()
    loads[0].wait()
    pl.semaphore_wait(barrier, len(peers))

    sent = []

    def w_copy(index, send_sem, device):
        return pltpu.make_async_remote_copy(
            src_ref=block(index),
            dst_ref=block(index),
            send_sem=send_sem,
            recv_sem=w_recv.at[index],
            device_id=device,
            device_id_type=pl.DeviceIdType.MESH,
        )

    def w_to(index, device):
        copy = w_copy(index, w_send.at[len(sent)], device)
        copy.start()
        sent.append(copy)

    def w_wait(index):
        w_copy(index, w_send.at[0], core).wait_recv()

    beside_x = (x_right, x_left, core)
    for peer in y_peers:
        w_to(d, peer)
    for p, peer in enumerate(beside_x):
        w_copy(d, f_send.at[y, p], peer).start()

    own_count = count[d]

    def live(k):
        return jnp.clip(own_count - k, 0, 1).astype(F32)

    loads[1].wait()
    for k in range(SEQS):
        rows = tok[ids[0, k]].astype(F32) * live(k)
        pick[k * L : (k + 1) * L, :] = rows.astype(BF16)
    loads[2].wait()

    c_copies = []

    def grad_piece(j):
        product = lax.dot_general(
            cot[:, j * 256 : (j + 1) * 256], pick[...], TN, preferred_element_type=F32
        )
        product = (product * factor).astype(BF16).reshape(4, 2, 32, 512)
        for cc in range(2):
            grad[cc, j] = product[:, cc]
        c_copies.append(
            send(grad.at[1 - c, j], from_core.at[j], c_send.at[j], c_recv.at[j], core)
        )

    def along_x(j):
        @pl.when(j != y)
        def _():
            w_wait(at(j, x, c))
            for p, peer in enumerate(beside_x):
                w_copy(at(j, x, c), f_send.at[j, p], peer).start()

    def around_x(j):
        from_l, from_r = at(j, xl, c), at(j, xr, c)
        w_wait(from_l)
        if j % 2 == 0:
            w_to(from_l, x_right)
        w_to(from_l, core)
        w_wait(from_r)
        if j % 2 == 1:
            w_to(from_r, x_left)
        w_to(from_r, core)

    def across_x(j):
        w_wait(at(j, xo, c))
        w_to(at(j, xo, c), core)

    def chunk_here(j):
        for xx in range(4):
            w_wait(at(j, xx, 1 - c))

    grad_piece(0)
    for j in range(4):
        along_x(j)
    grad_piece(1)
    for j in range(4):
        around_x(j)

    width = 1024 // CHUNKS
    z_copies = {}
    h_copies = []

    def z_right(j, r, src, dst):
        z_copies[0, j, r] = send(src, dst, z_send.at[0, j, r], z_recv.at[0, j, r], right)

    def z_left(j, r, src, dst):
        z_copies[1, j, r] = send(src, dst, z_send.at[1, j, r], z_recv.at[1, j, r], left)

    def start_chunk(j):
        for h in range(2):
            product = lax.dot_general(
                tok[h * 4 : (h + 1) * 4].reshape(512, 512),
                w[j * width : (j + 1) * width, :],
                NT,
                preferred_element_type=F32,
            )
            part[j, :, h] = product.astype(BF16).reshape(8, 64, width)
        far, near_r, near_l = (z + 4) % 8, (z + 3) % 8, (z + 5) % 8
        z_right(j, 0, part.at[j, far, 0], from_left.at[j, 0, 0])
        z_left(j, 0, part.at[j, far, 1], from_right.at[j, 0, 1])
        z_right(j, 4, part.at[j, near_r, 1], from_left.at[j, 1, 1])
        z_left(j, 4, part.at[j, near_l, 0], from_right.at[j, 1, 0])

    def add_into(ref, index, other):
        ref[index] = (ref[index].astype(F32) + other.astype(F32)).astype(BF16)

    def z_first(j):
        to_right, to_left = (z + 3) % 8, (z + 5) % 8
        z_copies[0, j, 0].wait_recv()
        add_into(part, (j, to_right, 0), from_left[j, 0, 0])
        z_right(j, 1, part.at[j, to_right, 0], from_left.at[j, 1, 0])
        z_copies[1, j, 0].wait_recv()
        add_into(part, (j, to_left, 1), from_right[j, 0, 1])
        z_left(j, 1, part.at[j, to_left, 1], from_right.at[j, 1, 1])

    def z_round(j, r):
        to_right, to_left = (z + 4 - r) % 8, (z + 4 + r) % 8
        z_copies[0, j, r - 1].wait_recv()
        if r == 2:
            z_copies[0, j, 4].wait_recv()
        add_into(part, (j, to_right), from_left[j, r - 1])
        z_right(j, r, part.at[j, to_right], from_left.at[j, r])
        z_copies[1, j, r - 1].wait_recv()
        if r == 2:
            z_copies[1, j, 4].wait_recv()
        add_into(part, (j, to_left), from_right[j, r - 1])
        z_left(j, r, part.at[j, to_left], from_right.at[j, r])

    def z_finish(j):
        z_copies[0, j, 3].wait_recv()
        z_copies[1, j, 3].wait_recv()
        total = part[j, z].astype(F32) + from_left[j, 3].astype(F32) + from_right[j, 3].astype(F32)
        kept[j] = total
        both[j] = total.astype(BF16)
        h_copies.append(
            send(both.at[j, 1 - half], from_half.at[j], h_send.at[j], h_recv.at[j], other_half)
        )

    def kv_finish(j):
        h_copies[j].wait_recv()
        total = kept[j, half] + from_half[j].astype(F32)
        kv_out[:, j * width : (j + 1) * width] = total.astype(BF16)

    x1_copies = {}
    x2_copies = {}
    y_copies = []

    def grad_core():
        for j in range(4):
            c_copies[j].wait_recv()
            add_into(grad, (c, j), from_core[j])
        for j in range(4):
            x1_copies[j] = send(
                grad.at[c, j, xo],
                x1.at[j],
                x1_send.at[j],
                x1_recv.at[j],
                x_right if j < 2 else x_left,
            )
        for j in (2, 3):
            x2_copies[0, j] = send(
                grad.at[c, j, xr], x2r.at[j], x2_send.at[0, j], x2_recv.at[0, j], x_right
            )
        for j in (0, 1):
            x2_copies[1, j] = send(
                grad.at[c, j, xl], x2l.at[j], x2_send.at[1, j], x2_recv.at[1, j], x_left
            )

    def grad_x():
        for j in range(2):
            x1_copies[j].wait_recv()
            add_into(grad, (c, j, xr), x1[j])
            x2_copies[0, j] = send(
                grad.at[c, j, xr], x2r.at[j], x2_send.at[0, j], x2_recv.at[0, j], x_right
            )
        for j in range(2, 4):
            x1_copies[j].wait_recv()
            add_into(grad, (c, j, xl), x1[j])
            x2_copies[1, j] = send(
                grad.at[c, j, xl], x2l.at[j], x2_send.at[1, j], x2_recv.at[1, j], x_left
            )

    def grad_y():
        for j in range(4):
            x2_copies[0, j].wait_recv()
            x2_copies[1, j].wait_recv()
        for j in range(4):
            total = grad[c, j, x].astype(F32) + x2r[j].astype(F32) + x2l[j].astype(F32)
            ysum[j] = total.astype(BF16)
        for k in range(1, 4):
            y_copies.append(
                send(
                    ysum.at[ys[k]],
                    from_y.at[k - 1],
                    y_send.at[k - 1],
                    y_recv.at[k - 1],
                    y_peers[k - 1],
                )
            )

    def grad_finish():
        total = ysum[y].astype(F32)
        for k in range(3):
            y_copies[k].wait_recv()
            total = total + from_y[k].astype(F32)
        wg_out[...] = total

    tg_copies = []

    def token_piece(p):
        rows = slice(p * 256, (p + 1) * 256)
        product = jnp.dot(cot[rows, :], w[...], preferred_element_type=F32)
        for i in range(2):
            own = product[i * L : (i + 1) * L] * live(2 * p + i)
            tg[p * 256 + i * L : p * 256 + (i + 1) * L, :] = own.astype(BF16)
        copy = pltpu.make_async_copy(tg.at[rows, :], tg_hbm.at[rows, :], tg_sem.at[p])
        copy.start()
        tg_copies.append(copy)

    across_x(0)
    across_x(1)
    for j in range(CHUNKS):
        chunk_here(j)
        start_chunk(j)
        if j + 2 < CHUNKS:
            across_x(j + 2)
    for j in range(CHUNKS):
        z_first(j)
    grad_piece(2)
    grad_piece(3)
    z_round(0, 2)
    z_round(1, 2)
    grad_core()
    z_round(2, 2)
    z_round(3, 2)
    token_piece(0)
    z_round(0, 3)
    grad_x()
    z_round(1, 3)
    token_piece(1)
    z_round(2, 3)
    grad_y()
    z_round(3, 3)
    z_finish(0)
    token_piece(2)
    z_finish(1)
    token_piece(3)
    z_finish(2)
    grad_finish()
    z_finish(3)
    for j in range(CHUNKS):
        kv_finish(j)

    for j in range(4):
        for p in range(3):
            w_copy(d, f_send.at[j, p], core).wait_send()
    everything = [*sent, *c_copies, *z_copies.values(), *h_copies]
    everything += [*x1_copies.values(), *x2_copies.values(), *y_copies]
    for copy in everything:
        copy.wait_send()
    for copy in tg_copies:
        copy.wait()


def per_device(tokens, weight_t, cotangent, hard_ids, hard_count):
    factor = 1.0 / math.sqrt(lax.axis_size("dp") * HARD_DEV * L)
    rows, width = tokens.shape
    chans = cotangent.shape[1]
    wide = chans // CHUNKS
    any_spec = pl.BlockSpec(memory_space=pl.ANY)
    smem = pl.BlockSpec(memory_space=pltpu.SMEM)
    vmem = pl.BlockSpec(memory_space=pltpu.VMEM)
    dma = pltpu.SemaphoreType.DMA

    def body(*refs):
        kernel(factor, *refs)

    return pl.pallas_call(
        body,
        out_shape=(
            jax.ShapeDtypeStruct((64, chans), BF16),
            jax.ShapeDtypeStruct((rows, width), BF16),
            jax.ShapeDtypeStruct((32, width), F32),
        ),
        in_specs=[smem, smem, any_spec, any_spec, any_spec],
        out_specs=(vmem, any_spec, vmem),
        scratch_shapes=[
            pltpu.VMEM((SEQS, L, width), BF16),
            pltpu.VMEM((rows, chans), BF16),
            pltpu.VMEM((chans, width), BF16),
            pltpu.VMEM((rows, width), BF16),
            pltpu.VMEM((CHUNKS, 8, 2, 64, wide), BF16),
            pltpu.VMEM((CHUNKS, 4, 2, 64, wide), BF16),
            pltpu.VMEM((CHUNKS, 4, 2, 64, wide), BF16),
            pltpu.VMEM((CHUNKS, 2, 64, wide), BF16),
            pltpu.VMEM((CHUNKS, 2, 64, wide), F32),
            pltpu.VMEM((CHUNKS, 64, wide), BF16),
            pltpu.VMEM((2, 4, 4, 32, width), BF16),
            pltpu.VMEM((4, 4, 32, width), BF16),
            pltpu.VMEM((4, 32, width), BF16),
            pltpu.VMEM((4, 32, width), BF16),
            pltpu.VMEM((4, 32, width), BF16),
            pltpu.VMEM((4, 32, width), BF16),
            pltpu.VMEM((3, 32, width), BF16),
            pltpu.VMEM((rows, width), BF16),
            dma((3,)),
            dma((4,)),
            dma((19,)),
            dma((4, 3)),
            dma((32,)),
            dma((2, CHUNKS, 5)),
            dma((2, CHUNKS, 5)),
            dma((CHUNKS,)),
            dma((CHUNKS,)),
            dma((4,)),
            dma((4,)),
            dma((4,)),
            dma((4,)),
            dma((2, 4)),
            dma((2, 4)),
            dma((3,)),
            dma((3,)),
        ],
        compiler_params=pltpu.CompilerParams(collective_id=0, has_side_effects=True),
    )(hard_ids, hard_count, tokens.reshape(SEQS, L, width), weight_t, cotangent)


def solution(mesh):
    return jax.shard_map(
        per_device,
        mesh=mesh,
        in_specs=(P("dp", "shard"), P("dp", "shard"), P("dp", None), P("dp", None), P()),
        out_specs=(P(("dp", "shard"), None), P("dp", "shard"), P("dp", "shard")),
        check_vma=False,
    )
```

```python
import math

import jax
import jax.numpy as jnp
from jax import lax
from jax.experimental import pallas as pl
from jax.experimental.pallas import tpu as pltpu
from jax.sharding import PartitionSpec as P

SEQS = 8
L = 128
HARD_DEV = 4
CHUNKS = 4
NT = (((1,), (1,)), ((), ()))
TN = (((0,), (0,)), ((), ()))
F32 = jnp.float32
BF16 = jnp.bfloat16


def send(src, dst, send_sem, recv_sem, device):
    copy = pltpu.make_async_remote_copy(
        src_ref=src,
        dst_ref=dst,
        send_sem=send_sem,
        recv_sem=recv_sem,
        device_id=device,
        device_id_type=pl.DeviceIdType.MESH,
    )
    copy.start()
    return copy


def kernel(
    factor,
    ids_hbm,
    count_hbm,
    tok_hbm,
    w_hbm,
    cot_hbm,
    kv_out,
    tg,
    wg_out,
    ids,
    count,
    tok,
    cot,
    w,
    pick,
    part,
    from_left,
    from_right,
    both,
    from_half,
    grad,
    from_core,
    x1,
    x2r,
    x2l,
    ysum,
    from_y,
    load_sem,
    w_send,
    f_send,
    w_recv,
    z_send,
    z_recv,
    h_send,
    h_recv,
    c_send,
    c_recv,
    x1_send,
    x1_recv,
    x2_send,
    x2_recv,
    y_send,
    y_recv,
):
    d = lax.axis_index("dp")
    s = lax.axis_index("shard")
    c = d % 2
    x = (d // 2) % 4
    y = d // 8
    z = s % 8
    half = s // 8
    xr, xl, xo = (x + 1) % 4, (x + 3) % 4, (x + 2) % 4
    right = (d, half * 8 + (z + 1) % 8)
    left = (d, half * 8 + (z + 7) % 8)
    other_half = (d, (1 - half) * 8 + z)

    def at(yy, xx, cc):
        return (yy * 4 + xx) * 2 + cc

    core = (at(y, x, 1 - c), s)
    x_right = (at(y, xr, c), s)
    x_left = (at(y, xl, c), s)
    ys = [(y + k) % 4 for k in range(4)]
    y_peers = [(at(ys[k], x, c), s) for k in range(1, 4)]

    barrier = pltpu.get_barrier_semaphore()
    peers = [*y_peers, x_right, x_left, core, right, left, other_half]
    for peer in peers:
        pl.semaphore_signal(barrier, inc=1, device_id=peer, device_id_type=pl.DeviceIdType.MESH)

    def block(index):
        return w.at[pl.ds(pl.multiple_of(index * 32, 32), 32), :]

    loads = [
        pltpu.make_async_copy(w_hbm, block(d), load_sem.at[0]),
        pltpu.make_async_copy(tok_hbm, tok, load_sem.at[1]),
        pltpu.make_async_copy(cot_hbm, cot, load_sem.at[2]),
        pltpu.make_async_copy(ids_hbm, ids, load_sem.at[3]),
        pltpu.make_async_copy(count_hbm, count, load_sem.at[4]),
    ]
    for load in loads:
        load.start()
    loads[0].wait()
    pl.semaphore_wait(barrier, len(peers))

    sent = []

    def w_copy(index, send_sem, device):
        return pltpu.make_async_remote_copy(
            src_ref=block(index),
            dst_ref=block(index),
            send_sem=send_sem,
            recv_sem=w_recv.at[index],
            device_id=device,
            device_id_type=pl.DeviceIdType.MESH,
        )

    def w_to(index, device):
        copy = w_copy(index, w_send.at[len(sent)], device)
        copy.start()
        sent.append(copy)

    def w_wait(index):
        w_copy(index, w_send.at[0], core).wait_recv()

    beside_x = (x_right, x_left, core)
    for peer in y_peers:
        w_to(d, peer)
    for p, peer in enumerate(beside_x):
        w_copy(d, f_send.at[y, p], peer).start()

    loads[3].wait()
    loads[4].wait()
    own_count = count[d]

    def live(k):
        return jnp.clip(own_count - k, 0, 1).astype(F32)

    loads[1].wait()
    for k in range(SEQS):
        rows = tok[ids[0, k]].astype(F32) * live(k)
        pick[k * L : (k + 1) * L, :] = rows.astype(BF16)
    loads[2].wait()

    c_copies = []

    def grad_piece(j):
        product = lax.dot_general(
            cot[:, j * 256 : (j + 1) * 256], pick[...], TN, preferred_element_type=F32
        )
        product = (product * factor).astype(BF16).reshape(4, 2, 32, 512)
        for cc in range(2):
            grad[cc, j] = product[:, cc]
        c_copies.append(
            send(grad.at[1 - c, j], from_core.at[j], c_send.at[j], c_recv.at[j], core)
        )

    def along_x(j):
        @pl.when(j != y)
        def _():
            w_wait(at(j, x, c))
            for p, peer in enumerate(beside_x):
                w_copy(at(j, x, c), f_send.at[j, p], peer).start()

    def around_x(j):
        from_l, from_r = at(j, xl, c), at(j, xr, c)
        w_wait(from_l)
        if j % 2 == 0:
            w_to(from_l, x_right)
        w_to(from_l, core)
        w_wait(from_r)
        if j % 2 == 1:
            w_to(from_r, x_left)
        w_to(from_r, core)

    def across_x(j):
        w_wait(at(j, xo, c))
        w_to(at(j, xo, c), core)

    def chunk_here(j):
        for xx in range(4):
            w_wait(at(j, xx, 1 - c))

    grad_piece(0)
    for j in range(4):
        along_x(j)
    grad_piece(1)
    around_x(0)
    around_x(1)
    grad_piece(2)
    around_x(2)
    around_x(3)
    grad_piece(3)

    width = 1024 // CHUNKS
    z_copies = {}
    h_copies = []

    def z_right(j, r, src, dst):
        z_copies[0, j, r] = send(src, dst, z_send.at[0, j, r], z_recv.at[0, j, r], right)

    def z_left(j, r, src, dst):
        z_copies[1, j, r] = send(src, dst, z_send.at[1, j, r], z_recv.at[1, j, r], left)

    def start_chunk(j):
        for h in range(2):
            product = lax.dot_general(
                tok[h * 4 : (h + 1) * 4].reshape(512, 512),
                w[j * width : (j + 1) * width, :],
                NT,
                preferred_element_type=F32,
            )
            part[j, :, h] = product.astype(BF16).reshape(8, 64, width)
        far, near_r, near_l = (z + 4) % 8, (z + 3) % 8, (z + 5) % 8
        z_right(j, 0, part.at[j, far, 0], from_left.at[j, 0, 0])
        z_left(j, 0, part.at[j, far, 1], from_right.at[j, 0, 1])
        z_right(j, 4, part.at[j, near_r, 1], from_left.at[j, 1, 1])
        z_left(j, 4, part.at[j, near_l, 0], from_right.at[j, 1, 0])

    def add_into(ref, index, other):
        ref[index] = (ref[index].astype(F32) + other.astype(F32)).astype(BF16)

    def z_first(j):
        to_right, to_left = (z + 3) % 8, (z + 5) % 8
        z_copies[0, j, 0].wait_recv()
        add_into(part, (j, to_right, 0), from_left[j, 0, 0])
        z_right(j, 1, part.at[j, to_right, 0], from_left.at[j, 1, 0])
        z_copies[1, j, 0].wait_recv()
        add_into(part, (j, to_left, 1), from_right[j, 0, 1])
        z_left(j, 1, part.at[j, to_left, 1], from_right.at[j, 1, 1])

    away = 1 - half

    def z_step(j, r, h, last, this):
        to_right, to_left = (z + 4 - r) % 8, (z + 4 + r) % 8
        for index in last:
            z_copies[0, j, index].wait_recv()
        add_into(part, (j, to_right, h), from_left[j, r - 1, h])
        z_right(j, this, part.at[j, to_right, h], from_left.at[j, r, h])
        for index in last:
            z_copies[1, j, index].wait_recv()
        add_into(part, (j, to_left, h), from_right[j, r - 1, h])
        z_left(j, this, part.at[j, to_left, h], from_right.at[j, r, h])

    def second_away(j):
        z_step(j, 2, away, (1, 4), 2)

    def second_own(j):
        z_step(j, 2, half, (), 5)

    def third_away(j):
        z_step(j, 3, away, (2,), 3)

    def third_own(j):
        z_step(j, 3, half, (5,), 6)

    def z_total(j, h, index):
        z_copies[0, j, index].wait_recv()
        z_copies[1, j, index].wait_recv()
        total = part[j, z, h].astype(F32) + from_left[j, 3, h].astype(F32)
        return total + from_right[j, 3, h].astype(F32)

    def to_other_half(j):
        both[j] = z_total(j, away, 3).astype(BF16)
        h_copies.append(
            send(both.at[j], from_half.at[j], h_send.at[j], h_recv.at[j], other_half)
        )

    def kv_finish(j):
        total = z_total(j, half, 6)
        h_copies[j].wait_recv()
        total = total + from_half[j].astype(F32)
        kv_out[:, j * width : (j + 1) * width] = total.astype(BF16)

    x1_copies = {}
    x2_copies = {}
    y_copies = []

    def grad_core():
        for j in range(4):
            c_copies[j].wait_recv()
            add_into(grad, (c, j), from_core[j])
        for j in range(4):
            x1_copies[j] = send(
                grad.at[c, j, xo],
                x1.at[j],
                x1_send.at[j],
                x1_recv.at[j],
                x_right if j < 2 else x_left,
            )
        for j in (2, 3):
            x2_copies[0, j] = send(
                grad.at[c, j, xr], x2r.at[j], x2_send.at[0, j], x2_recv.at[0, j], x_right
            )
        for j in (0, 1):
            x2_copies[1, j] = send(
                grad.at[c, j, xl], x2l.at[j], x2_send.at[1, j], x2_recv.at[1, j], x_left
            )

    def grad_x():
        for j in range(2):
            x1_copies[j].wait_recv()
            add_into(grad, (c, j, xr), x1[j])
            x2_copies[0, j] = send(
                grad.at[c, j, xr], x2r.at[j], x2_send.at[0, j], x2_recv.at[0, j], x_right
            )
        for j in range(2, 4):
            x1_copies[j].wait_recv()
            add_into(grad, (c, j, xl), x1[j])
            x2_copies[1, j] = send(
                grad.at[c, j, xl], x2l.at[j], x2_send.at[1, j], x2_recv.at[1, j], x_left
            )

    def grad_y():
        for j in range(4):
            x2_copies[0, j].wait_recv()
            x2_copies[1, j].wait_recv()
        for j in range(4):
            total = grad[c, j, x].astype(F32) + x2r[j].astype(F32) + x2l[j].astype(F32)
            ysum[j] = total.astype(BF16)
        for k in range(1, 4):
            y_copies.append(
                send(
                    ysum.at[ys[k]],
                    from_y.at[k - 1],
                    y_send.at[k - 1],
                    y_recv.at[k - 1],
                    y_peers[k - 1],
                )
            )

    def grad_finish():
        total = ysum[y].astype(F32)
        for k in range(3):
            y_copies[k].wait_recv()
            total = total + from_y[k].astype(F32)
        wg_out[...] = total

    def token_piece(p):
        rows = slice(p * 256, (p + 1) * 256)
        product = jnp.dot(cot[rows, :], w[...], preferred_element_type=F32)
        for i in range(2):
            own = product[i * L : (i + 1) * L] * live(2 * p + i)
            tg[p * 256 + i * L : p * 256 + (i + 1) * L, :] = own.astype(BF16)

    across_x(0)
    across_x(1)
    for j in range(CHUNKS):
        chunk_here(j)
        start_chunk(j)
        if j + 2 < CHUNKS:
            across_x(j + 2)
    for j in range(CHUNKS):
        z_first(j)
    grad_core()
    for j in range(CHUNKS):
        second_away(j)
    token_piece(0)
    grad_x()
    for j in range(CHUNKS):
        second_own(j)
    token_piece(1)
    third_away(0)
    third_away(1)
    grad_y()
    third_away(2)
    third_away(3)
    token_piece(2)
    third_own(0)
    to_other_half(0)
    third_own(1)
    to_other_half(1)
    third_own(2)
    to_other_half(2)
    third_own(3)
    to_other_half(3)
    token_piece(3)
    grad_finish()
    for j in range(CHUNKS):
        kv_finish(j)

    for j in range(4):
        for p in range(3):
            w_copy(d, f_send.at[j, p], core).wait_send()
    everything = [*sent, *c_copies, *z_copies.values(), *h_copies]
    everything += [*x1_copies.values(), *x2_copies.values(), *y_copies]
    for copy in everything:
        copy.wait_send()


def per_device(tokens, weight_t, cotangent, hard_ids, hard_count):
    factor = 1.0 / math.sqrt(lax.axis_size("dp") * HARD_DEV * L)
    rows, width = tokens.shape
    chans = cotangent.shape[1]
    wide = chans // CHUNKS
    any_spec = pl.BlockSpec(memory_space=pl.ANY)
    vmem = pl.BlockSpec(memory_space=pltpu.VMEM)
    dma = pltpu.SemaphoreType.DMA

    def body(*refs):
        kernel(factor, *refs)

    return pl.pallas_call(
        body,
        out_shape=(
            pltpu.VMEM((64, chans), BF16),
            pltpu.VMEM((rows, width), BF16),
            pltpu.VMEM((32, width), F32),
        ),
        in_specs=[any_spec] * 5,
        out_specs=(vmem, vmem, vmem),
        scratch_shapes=[
            pltpu.SMEM((1, SEQS), jnp.int32),
            pltpu.SMEM(hard_count.shape, jnp.int32),
            pltpu.VMEM((SEQS, L, width), BF16),
            pltpu.VMEM((rows, chans), BF16),
            pltpu.VMEM((chans, width), BF16),
            pltpu.VMEM((rows, width), BF16),
            pltpu.VMEM((CHUNKS, 8, 2, 64, wide), BF16),
            pltpu.VMEM((CHUNKS, 4, 2, 64, wide), BF16),
            pltpu.VMEM((CHUNKS, 4, 2, 64, wide), BF16),
            pltpu.VMEM((CHUNKS, 64, wide), BF16),
            pltpu.VMEM((CHUNKS, 64, wide), BF16),
            pltpu.VMEM((2, 4, 4, 32, width), BF16),
            pltpu.VMEM((4, 4, 32, width), BF16),
            pltpu.VMEM((4, 32, width), BF16),
            pltpu.VMEM((4, 32, width), BF16),
            pltpu.VMEM((4, 32, width), BF16),
            pltpu.VMEM((4, 32, width), BF16),
            pltpu.VMEM((3, 32, width), BF16),
            dma((5,)),
            dma((19,)),
            dma((4, 3)),
            dma((32,)),
            dma((2, CHUNKS, 7)),
            dma((2, CHUNKS, 7)),
            dma((CHUNKS,)),
            dma((CHUNKS,)),
            dma((4,)),
            dma((4,)),
            dma((4,)),
            dma((4,)),
            dma((2, 4)),
            dma((2, 4)),
            dma((3,)),
            dma((3,)),
        ],
        compiler_params=pltpu.CompilerParams(collective_id=0, has_side_effects=True),
    )(hard_ids, hard_count, tokens.reshape(SEQS, L, width), weight_t, cotangent)


def solution(mesh):
    return jax.shard_map(
        per_device,
        mesh=mesh,
        in_specs=(P("dp", "shard"), P("dp", "shard"), P("dp", None), P("dp", None), P()),
        out_specs=(P(("dp", "shard"), None), P("dp", "shard"), P("dp", "shard")),
        check_vma=False,
    )
```

```python
import math

import jax
import jax.numpy as jnp
from jax import lax
from jax.experimental import pallas as pl
from jax.experimental.pallas import tpu as pltpu
from jax.sharding import PartitionSpec as P

SEQS = 8
L = 128
HARD_DEV = 4
CHUNKS = 4
NT = (((1,), (1,)), ((), ()))
TN = (((0,), (0,)), ((), ()))
F32 = jnp.float32
BF16 = jnp.bfloat16


def send(src, dst, send_sem, recv_sem, device):
    copy = pltpu.make_async_remote_copy(
        src_ref=src,
        dst_ref=dst,
        send_sem=send_sem,
        recv_sem=recv_sem,
        device_id=device,
        device_id_type=pl.DeviceIdType.MESH,
    )
    copy.start()
    return copy


def kernel(
    factor,
    ids_hbm,
    count_hbm,
    tok_hbm,
    w_hbm,
    cot_hbm,
    kv_out,
    tg,
    wg_out,
    ids,
    count,
    tok,
    cot,
    w,
    pick,
    part,
    from_left,
    from_right,
    both,
    from_half,
    grad,
    from_core,
    x1,
    x2r,
    x2l,
    ysum,
    from_y,
    load_sem,
    w_send,
    f_send,
    w_recv,
    z_send,
    z_recv,
    h_send,
    h_recv,
    c_send,
    c_recv,
    x1_send,
    x1_recv,
    x2_send,
    x2_recv,
    y_send,
    y_recv,
):
    d = lax.axis_index("dp")
    s = lax.axis_index("shard")
    c = d % 2
    x = (d // 2) % 4
    y = d // 8
    z = s % 8
    half = s // 8
    xr, xl, xo = (x + 1) % 4, (x + 3) % 4, (x + 2) % 4
    right = (d, half * 8 + (z + 1) % 8)
    left = (d, half * 8 + (z + 7) % 8)
    other_half = (d, (1 - half) * 8 + z)

    def at(yy, xx, cc):
        return (yy * 4 + xx) * 2 + cc

    core = (at(y, x, 1 - c), s)
    x_right = (at(y, xr, c), s)
    x_left = (at(y, xl, c), s)
    ys = [(y + k) % 4 for k in range(4)]
    y_peers = [(at(ys[k], x, c), s) for k in range(1, 4)]

    barrier = pltpu.get_barrier_semaphore()
    peers = [*y_peers, x_right, x_left, core, right, left, other_half]
    for peer in peers:
        pl.semaphore_signal(barrier, inc=1, device_id=peer, device_id_type=pl.DeviceIdType.MESH)

    def block(index):
        return w.at[pl.ds(pl.multiple_of(index * 32, 32), 32), :]

    loads = [
        pltpu.make_async_copy(w_hbm, block(d), load_sem.at[0]),
        pltpu.make_async_copy(tok_hbm, tok, load_sem.at[1]),
        pltpu.make_async_copy(cot_hbm, cot, load_sem.at[2]),
        pltpu.make_async_copy(ids_hbm, ids, load_sem.at[3]),
        pltpu.make_async_copy(count_hbm, count, load_sem.at[4]),
    ]
    for load in loads:
        load.start()
    loads[0].wait()
    pl.semaphore_wait(barrier, len(peers))

    sent = []

    def w_copy(index, send_sem, device):
        return pltpu.make_async_remote_copy(
            src_ref=block(index),
            dst_ref=block(index),
            send_sem=send_sem,
            recv_sem=w_recv.at[index],
            device_id=device,
            device_id_type=pl.DeviceIdType.MESH,
        )

    def w_to(index, device):
        copy = w_copy(index, w_send.at[len(sent)], device)
        copy.start()
        sent.append(copy)

    def w_wait(index):
        w_copy(index, w_send.at[0], core).wait_recv()

    beside_x = (x_right, x_left, core)
    for peer in y_peers:
        w_to(d, peer)
    for p, peer in enumerate(beside_x):
        w_copy(d, f_send.at[y, p], peer).start()

    loads[3].wait()
    loads[4].wait()
    own_count = count[d]

    def live(k):
        return jnp.clip(own_count - k, 0, 1).astype(F32)

    loads[1].wait()
    for k in range(SEQS):
        rows = tok[ids[0, k]].astype(F32) * live(k)
        pick[k * L : (k + 1) * L, :] = rows.astype(BF16)
    loads[2].wait()

    c_copies = []

    def grad_piece(j):
        product = lax.dot_general(
            cot[:, j * 256 : (j + 1) * 256], pick[...], TN, preferred_element_type=F32
        )
        product = (product * factor).astype(BF16).reshape(4, 2, 32, 512)
        for cc in range(2):
            grad[cc, j] = product[:, cc]
        c_copies.append(
            send(grad.at[1 - c, j], from_core.at[j], c_send.at[j], c_recv.at[j], core)
        )

    def along_x(j):
        @pl.when(j != y)
        def _():
            w_wait(at(j, x, c))
            for p, peer in enumerate(beside_x):
                w_copy(at(j, x, c), f_send.at[j, p], peer).start()

    def around_x(j):
        from_l, from_r = at(j, xl, c), at(j, xr, c)
        w_wait(from_l)
        if j % 2 == 0:
            w_to(from_l, x_right)
        w_to(from_l, core)
        w_wait(from_r)
        if j % 2 == 1:
            w_to(from_r, x_left)
        w_to(from_r, core)

    def across_x(j):
        w_wait(at(j, xo, c))
        w_to(at(j, xo, c), core)

    def chunk_here(j):
        for xx in range(4):
            w_wait(at(j, xx, 1 - c))

    grad_piece(0)
    for j in range(4):
        along_x(j)
    grad_piece(1)
    around_x(0)
    around_x(1)
    grad_piece(2)
    around_x(2)
    around_x(3)
    grad_piece(3)

    width = 1024 // CHUNKS
    z_copies = {}
    h_copies = []

    def z_right(j, r, src, dst):
        z_copies[0, j, r] = send(src, dst, z_send.at[0, j, r], z_recv.at[0, j, r], right)

    def z_left(j, r, src, dst):
        z_copies[1, j, r] = send(src, dst, z_send.at[1, j, r], z_recv.at[1, j, r], left)

    def start_chunk(j):
        for h in range(2):
            product = lax.dot_general(
                tok[h * 4 : (h + 1) * 4].reshape(512, 512),
                w[j * width : (j + 1) * width, :],
                NT,
                preferred_element_type=F32,
            )
            part[j, :, h] = product.astype(BF16).reshape(8, 64, width)
        far, near_r, near_l = (z + 4) % 8, (z + 3) % 8, (z + 5) % 8
        z_right(j, 0, part.at[j, far, 0], from_left.at[j, 0, 0])
        z_left(j, 0, part.at[j, far, 1], from_right.at[j, 0, 1])
        z_right(j, 4, part.at[j, near_r, 1], from_left.at[j, 1, 1])
        z_left(j, 4, part.at[j, near_l, 0], from_right.at[j, 1, 0])

    def add_into(ref, index, other):
        ref[index] = (ref[index].astype(F32) + other.astype(F32)).astype(BF16)

    def z_first(j):
        to_right, to_left = (z + 3) % 8, (z + 5) % 8
        z_copies[0, j, 0].wait_recv()
        add_into(part, (j, to_right, 0), from_left[j, 0, 0])
        z_right(j, 1, part.at[j, to_right, 0], from_left.at[j, 1, 0])
        z_copies[1, j, 0].wait_recv()
        add_into(part, (j, to_left, 1), from_right[j, 0, 1])
        z_left(j, 1, part.at[j, to_left, 1], from_right.at[j, 1, 1])

    away = 1 - half

    def z_step(j, r, h, last, this):
        to_right, to_left = (z + 4 - r) % 8, (z + 4 + r) % 8
        for index in last:
            z_copies[0, j, index].wait_recv()
        add_into(part, (j, to_right, h), from_left[j, r - 1, h])
        z_right(j, this, part.at[j, to_right, h], from_left.at[j, r, h])
        for index in last:
            z_copies[1, j, index].wait_recv()
        add_into(part, (j, to_left, h), from_right[j, r - 1, h])
        z_left(j, this, part.at[j, to_left, h], from_right.at[j, r, h])

    def second_away(j):
        z_step(j, 2, away, (1, 4), 2)

    def second_own(j):
        z_step(j, 2, half, (), 5)

    def third_away(j):
        z_step(j, 3, away, (2,), 3)

    def third_own(j):
        z_step(j, 3, half, (5,), 6)

    def z_total(j, h, index):
        z_copies[0, j, index].wait_recv()
        z_copies[1, j, index].wait_recv()
        total = part[j, z, h].astype(F32) + from_left[j, 3, h].astype(F32)
        return total + from_right[j, 3, h].astype(F32)

    def to_other_half(j):
        both[j] = z_total(j, away, 3).astype(BF16)
        h_copies.append(
            send(both.at[j], from_half.at[j], h_send.at[j], h_recv.at[j], other_half)
        )

    def kv_finish(j):
        total = z_total(j, half, 6)
        h_copies[j].wait_recv()
        total = total + from_half[j].astype(F32)
        kv_out[:, j * width : (j + 1) * width] = total.astype(BF16)

    x1_copies = {}
    x2_copies = {}
    y_copies = []

    def grad_core():
        for j in range(4):
            c_copies[j].wait_recv()
            add_into(grad, (c, j), from_core[j])
        for j in range(4):
            x1_copies[j] = send(
                grad.at[c, j, xo],
                x1.at[j],
                x1_send.at[j],
                x1_recv.at[j],
                x_right if j < 2 else x_left,
            )
        for j in (2, 3):
            x2_copies[0, j] = send(
                grad.at[c, j, xr], x2r.at[j], x2_send.at[0, j], x2_recv.at[0, j], x_right
            )
        for j in (0, 1):
            x2_copies[1, j] = send(
                grad.at[c, j, xl], x2l.at[j], x2_send.at[1, j], x2_recv.at[1, j], x_left
            )

    def grad_x():
        for j in range(2):
            x1_copies[j].wait_recv()
            add_into(grad, (c, j, xr), x1[j])
            x2_copies[0, j] = send(
                grad.at[c, j, xr], x2r.at[j], x2_send.at[0, j], x2_recv.at[0, j], x_right
            )
        for j in range(2, 4):
            x1_copies[j].wait_recv()
            add_into(grad, (c, j, xl), x1[j])
            x2_copies[1, j] = send(
                grad.at[c, j, xl], x2l.at[j], x2_send.at[1, j], x2_recv.at[1, j], x_left
            )

    def grad_y():
        for j in range(4):
            x2_copies[0, j].wait_recv()
            x2_copies[1, j].wait_recv()
        for j in range(4):
            total = grad[c, j, x].astype(F32) + x2r[j].astype(F32) + x2l[j].astype(F32)
            ysum[j] = total.astype(BF16)
        for k in range(1, 4):
            y_copies.append(
                send(
                    ysum.at[ys[k]],
                    from_y.at[k - 1],
                    y_send.at[k - 1],
                    y_recv.at[k - 1],
                    y_peers[k - 1],
                )
            )

    def grad_finish():
        total = ysum[y].astype(F32)
        for k in range(3):
            y_copies[k].wait_recv()
            total = total + from_y[k].astype(F32)
        wg_out[...] = total

    def token_piece(p):
        rows = slice(p * 256, (p + 1) * 256)
        product = jnp.dot(cot[rows, :], w[...], preferred_element_type=F32)
        for i in range(2):
            own = product[i * L : (i + 1) * L] * live(2 * p + i)
            tg[p * 256 + i * L : p * 256 + (i + 1) * L, :] = own.astype(BF16)

    across_x(0)
    across_x(1)
    for j in range(CHUNKS):
        chunk_here(j)
        start_chunk(j)
        if j + 2 < CHUNKS:
            across_x(j + 2)
    for j in range(CHUNKS):
        z_first(j)
    grad_core()
    for j in range(CHUNKS):
        second_away(j)
    token_piece(0)
    grad_x()
    for j in range(CHUNKS):
        second_own(j)
    token_piece(1)
    third_away(0)
    third_away(1)
    grad_y()
    third_away(2)
    third_away(3)
    token_piece(2)
    third_own(0)
    to_other_half(0)
    third_own(1)
    to_other_half(1)
    third_own(2)
    to_other_half(2)
    third_own(3)
    to_other_half(3)
    token_piece(3)
    grad_finish()
    for j in range(CHUNKS):
        kv_finish(j)

    for j in range(4):
        for p in range(3):
            w_copy(d, f_send.at[j, p], core).wait_send()
    everything = [*sent, *c_copies, *z_copies.values(), *h_copies]
    everything += [*x1_copies.values(), *x2_copies.values(), *y_copies]
    for copy in everything:
        copy.wait_send()


def write_out(kv, tg, wg, kv_out, tg_out, wg_out, sem):
    pairs = [(tg, tg_out), (kv, kv_out), (wg, wg_out)]
    copies = [pltpu.make_async_copy(a, o, sem.at[i]) for i, (a, o) in enumerate(pairs)]
    for copy in copies:
        copy.start()
    for copy in copies:
        copy.wait()


def per_device(tokens, weight_t, cotangent, hard_ids, hard_count):
    factor = 1.0 / math.sqrt(lax.axis_size("dp") * HARD_DEV * L)
    rows, width = tokens.shape
    chans = cotangent.shape[1]
    wide = chans // CHUNKS
    any_spec = pl.BlockSpec(memory_space=pl.ANY)
    vmem = pl.BlockSpec(memory_space=pltpu.VMEM)
    dma = pltpu.SemaphoreType.DMA

    def body(*refs):
        kernel(factor, *refs)

    results = pl.pallas_call(
        body,
        out_shape=(
            pltpu.VMEM((64, chans), BF16),
            pltpu.VMEM((rows, width), BF16),
            pltpu.VMEM((32, width), F32),
        ),
        in_specs=[any_spec] * 5,
        out_specs=(vmem, vmem, vmem),
        scratch_shapes=[
            pltpu.SMEM((1, SEQS), jnp.int32),
            pltpu.SMEM(hard_count.shape, jnp.int32),
            pltpu.VMEM((SEQS, L, width), BF16),
            pltpu.VMEM((rows, chans), BF16),
            pltpu.VMEM((chans, width), BF16),
            pltpu.VMEM((rows, width), BF16),
            pltpu.VMEM((CHUNKS, 8, 2, 64, wide), BF16),
            pltpu.VMEM((CHUNKS, 4, 2, 64, wide), BF16),
            pltpu.VMEM((CHUNKS, 4, 2, 64, wide), BF16),
            pltpu.VMEM((CHUNKS, 64, wide), BF16),
            pltpu.VMEM((CHUNKS, 64, wide), BF16),
            pltpu.VMEM((2, 4, 4, 32, width), BF16),
            pltpu.VMEM((4, 4, 32, width), BF16),
            pltpu.VMEM((4, 32, width), BF16),
            pltpu.VMEM((4, 32, width), BF16),
            pltpu.VMEM((4, 32, width), BF16),
            pltpu.VMEM((4, 32, width), BF16),
            pltpu.VMEM((3, 32, width), BF16),
            dma((5,)),
            dma((19,)),
            dma((4, 3)),
            dma((32,)),
            dma((2, CHUNKS, 7)),
            dma((2, CHUNKS, 7)),
            dma((CHUNKS,)),
            dma((CHUNKS,)),
            dma((4,)),
            dma((4,)),
            dma((4,)),
            dma((4,)),
            dma((2, 4)),
            dma((2, 4)),
            dma((3,)),
            dma((3,)),
        ],
        compiler_params=pltpu.CompilerParams(collective_id=0, has_side_effects=True),
    )(hard_ids, hard_count, tokens.reshape(SEQS, L, width), weight_t, cotangent)
    results = [pltpu.with_memory_space_constraint(a, pltpu.VMEM) for a in results]
    return pl.pallas_call(
        write_out,
        out_shape=tuple(jax.ShapeDtypeStruct(a.shape, a.dtype) for a in results),
        in_specs=[vmem] * 3,
        out_specs=(any_spec,) * 3,
        scratch_shapes=[dma((3,))],
    )(*results)


def solution(mesh):
    return jax.shard_map(
        per_device,
        mesh=mesh,
        in_specs=(P("dp", "shard"), P("dp", "shard"), P("dp", None), P("dp", None), P()),
        out_specs=(P(("dp", "shard"), None), P("dp", "shard"), P("dp", "shard")),
        check_vma=False,
    )
```
